512 devices in a mesh: ctx: 64 (over z, y), head: 8 (over x, core).
Axes of the slice: x: 4, y: 4, z: 16, core: 2. Of those that a mesh axis runs over, the one named last changes fastest.
Arguments:
- tokens: bfloat16 [32768, 5376], P('ctx', 'head'), may hold values from -6 to 6
- pre_gain: float32 [5376], replicated, may hold values from 0.25 to 1.75
- post_gain: float32 [5376], replicated, may hold values from 0.25 to 1.75
- w_qkv: bfloat16 [5376, 4096], P('ctx', 'head')
- w_o: bfloat16 [2048, 5376], P('head', 'ctx')
- page_start: int32 [64], replicated, may hold values from 128 to 32512, as said below
- page_of: int32 [32768], P('ctx'), may hold values from -1 to 63, as said below
Outputs:
- mixed_out: bfloat16 [32768, 5376], P('ctx', 'head')
The draws below stay inside these ranges and needn't reach their ends.
Inputs may be any that keep to these rules, and one draw needn't show every extreme that they name: `page_start`: entry p lies from 2 p * 256 + 256/2 to 2 p * 256 + 3 * 128 and is at most 32512; pages never intersect. Slots that no position names are unused. page_of[t] = p exactly where t lies in the 256 positions from page_start[p] and slot p holds an image.
All inputs are finite; a program needn't handle non-finite values.
Results may differ from the reference program's by a relative error of at most 0.018.
Values may be sent and summed in bfloat16 or wider, within the bound.
A program may use at most 64 MiB of HBM per device.

```python
import math
import jax
import jax.numpy as jnp
from jax import lax

D = 5376
HD = 128
KVH = 8
GROUP = 2
WINDOW = 1024
PAGE = 256
TOK_DEV = 512
HQ = 16
TOKENS = 32768
PAGES = 64
NB = 2
N_CTX = 64
N_HEAD = 8


def draw_w_qkv(key, part):
    width_cols = KVH * (GROUP + 2) * HD
    base_draw = jax.random.normal(key, (D, width_cols), jnp.float32) * D ** (-0.5)
    return base_draw.astype(jnp.bfloat16)


def draw_w_o(key, part):
    height = KVH * GROUP * HD
    base_draw = jax.random.normal(key, (height, D), jnp.float32) * height ** (-0.5)
    col_frac = jnp.arange(D, dtype=jnp.float32) / D
    col_draw = jax.random.uniform(jax.random.fold_in(key, 5), (1, D), jnp.float32)
    col_scale = jnp.exp(0.5 * math.log(3.0) * col_frac[None, :] + 0.5 * math.log(10.0) * col_draw)
    return (base_draw * col_scale).astype(jnp.bfloat16)


def page_layout(key):
    base_key = jax.random.fold_in(key, 11)
    slot_ids = jnp.arange(PAGES, dtype=jnp.int32)
    slot_base = slot_ids * (2 * PAGE) + PAGE // 2
    offsets = jax.random.randint(jax.random.fold_in(base_key, 1), (PAGES,), 0, PAGE + 1)
    boundary = (slot_base + PAGE // 2 + TOK_DEV - 1) // TOK_DEV * TOK_DEV
    can_cross = boundary <= slot_ids * (2 * PAGE) + 2 * PAGE
    needed = (boundary == TOK_DEV) | (boundary == TOKENS // 2) | (boundary == TOKENS // 2 + TOK_DEV) | (boundary == TOKENS - TOK_DEV)
    needed = needed & can_cross
    coin = jax.random.randint(jax.random.fold_in(base_key, 3), (PAGES,), 0, 2)
    crossing = can_cross & ((coin == 1) | needed)
    starts = jnp.where(crossing, boundary - PAGE // 2, slot_base + offsets)
    starts = jnp.minimum(starts, TOKENS - PAGE).astype(jnp.int32)
    present = jax.random.randint(jax.random.fold_in(base_key, 2), (PAGES,), 0, 2)
    present = jnp.where(needed, 1, present)
    return (starts, present)


def draw_page_start(key, part):
    starts, present = page_layout(key)
    return starts


def draw_page_of(key, part):
    starts, present = page_layout(key)
    position = jnp.arange(TOKENS, dtype=jnp.int32)
    slot_table = jnp.arange(PAGES, dtype=jnp.int32)
    inside = (position[:, None] >= starts[None, :]) & (position[:, None] < starts[None, :] + PAGE) & (present[None, :] == 1)
    found = jnp.sum(jnp.where(inside, slot_table[None, :] + 1, 0), axis=1)
    return (found - 1).astype(jnp.int32)


def block_scale(own_key, extent, shards, smallest, high):
    def one(dim, parts):
        draws = jax.random.uniform(jax.random.fold_in(jax.random.fold_in(own_key, 6), dim), (parts,), jnp.float32, smallest / len(shards), high / len(shards))
        return jnp.repeat(jnp.exp(draws), extent[dim] // parts).reshape((-1,) + (1,) * (len(extent) - dim - 1))

    factor_of = one(*shards[0])
    for cut in shards[1:]:
        factor_of = factor_of * one(*cut)
    return factor_of


def noise(own_key, extent, deviation, reach, split=(), kind=jnp.bfloat16):
    level = block_scale(own_key, extent, split, -0.22, 0.18) if split else 1.0
    values = jax.random.normal(own_key, extent, jnp.float32) * deviation * level
    return jnp.minimum(jnp.maximum(values, -reach), reach).astype(kind)


def setup_inputs(seed: int = 0) -> dict:
    key_list = jax.random.split(jax.random.key(seed), 8)
    tokens = noise(key_list[0], (TOKENS, D), 1.0, 6.0, ((0, 64), (1, 8)))
    pre_gain = jnp.clip(1.0 + 0.15 * jax.random.normal(key_list[1], (D,), jnp.float32), 0.25, 1.75)
    post_gain = jnp.clip(1.0 + 0.15 * jax.random.normal(key_list[2], (D,), jnp.float32), 0.25, 1.75)
    w_qkv = draw_w_qkv(jax.random.fold_in(key_list[7], 71), 0)
    w_o = draw_w_o(jax.random.fold_in(key_list[7], 71), 0)
    page_start = draw_page_start(jax.random.fold_in(key_list[7], 71), 0)
    page_of = draw_page_of(jax.random.fold_in(key_list[7], 71), 0)
    return dict(tokens=tokens, pre_gain=pre_gain, post_gain=post_gain, w_qkv=w_qkv, w_o=w_o, page_start=page_start, page_of=page_of)


SCALE = 168.0 ** (-0.5)
EPS = 1e-06

def rms_scale(values, gain):
    mean_sq = lax.optimization_barrier(jnp.mean(values * values, axis=-1, keepdims=True))
    return values * lax.rsqrt(mean_sq + EPS) * gain.astype(jnp.float32)

def rotate(values, positions):
    half_dim = values.shape[-1] // 2
    inv_freq = 10000.0 ** (-2.0 * jnp.arange(half_dim, dtype=jnp.float32) / values.shape[-1])
    angles = positions.astype(jnp.float32)[:, None] * inv_freq[None, :]
    cosine = jnp.cos(angles)[:, None, :]
    sine_part = jnp.sin(angles)[:, None, :]
    first_half = values[..., :half_dim]
    second = values[..., half_dim:]
    return jnp.concatenate([first_half * cosine - second * sine_part, second * cosine + first_half * sine_part], axis=-1)

def allowed_mask(query_pos, key_pos, query_page, page_start):
    page_table = jnp.arange(page_start.shape[0], dtype=jnp.int32)
    first_pos = lax.optimization_barrier(jnp.sum(jnp.where(query_page[:, None] == page_table[None, :], page_start[None, :], 0), axis=1))
    in_window = (key_pos[None, :] <= query_pos[:, None]) & (query_pos[:, None] - key_pos[None, :] < WINDOW) & (key_pos[None, :] >= 0)
    inside = (query_page[:, None] >= 0) & (key_pos[None, :] >= first_pos[:, None]) & (key_pos[None, :] < first_pos[:, None] + PAGE)
    return in_window | inside

def attend(queries, key_block, value_block, mask):
    scores = jnp.einsum('tkgd,skd->kgts', queries.astype(jnp.float32), key_block.astype(jnp.float32)) * SCALE
    scores = jnp.where(mask[None, None], scores, -jnp.inf)
    row_max = lax.optimization_barrier(jnp.max(scores, axis=-1, keepdims=True))
    weights = jnp.exp(scores - row_max)
    probabilities = (weights / lax.optimization_barrier(jnp.sum(weights, axis=-1, keepdims=True))).astype(jnp.bfloat16)
    mixed_out = jnp.einsum('kgts,skd->tkgd', probabilities.astype(jnp.float32), value_block.astype(jnp.float32))
    return mixed_out.reshape(mixed_out.shape[0], -1).astype(jnp.bfloat16)

def reference(tokens, pre_gain, post_gain, w_qkv, w_o, page_start, page_of):
    tokens_f32 = tokens.astype(jnp.float32)
    normed = rms_scale(tokens_f32, pre_gain).astype(jnp.bfloat16)
    projected = jnp.dot(normed, w_qkv, preferred_element_type=jnp.float32).reshape(TOKENS, KVH, GROUP + 2, HD)
    positions = jnp.arange(TOKENS, dtype=jnp.int32)
    queries = rotate(projected[:, :, :GROUP].reshape(TOKENS, KVH * GROUP, HD), positions)
    queries = queries.reshape(TOKENS, KVH, GROUP, HD).astype(jnp.bfloat16)
    key_all = rotate(projected[:, :, GROUP], positions).astype(jnp.bfloat16)
    values = projected[:, :, GROUP + 1].astype(jnp.bfloat16)
    back_rows = NB * TOK_DEV
    key_span = (NB + 2) * TOK_DEV
    pad_keys = jnp.pad(key_all, ((back_rows, TOK_DEV), (0, 0), (0, 0)))
    pad_values = jnp.pad(values, ((back_rows, TOK_DEV), (0, 0), (0, 0)))

    def one_block(block_index):
        row_start = (block_index * TOK_DEV).astype(jnp.int32)
        query_block = lax.dynamic_slice_in_dim(queries, row_start, TOK_DEV, 0)
        key_block = lax.dynamic_slice_in_dim(pad_keys, row_start, key_span, 0)
        value_block = lax.dynamic_slice_in_dim(pad_values, row_start, key_span, 0)
        query_pos = row_start + jnp.arange(TOK_DEV, dtype=jnp.int32)
        key_pos = row_start - back_rows + jnp.arange(key_span, dtype=jnp.int32)
        page_block = lax.dynamic_slice_in_dim(page_of, row_start, TOK_DEV, 0)
        mask = allowed_mask(query_pos, key_pos, page_block, page_start)
        return attend(query_block, key_block, value_block, mask)
    attended = lax.map(one_block, jnp.arange(N_CTX, dtype=jnp.int32)).reshape(TOKENS, HQ * HD)
    group_rows = HQ * HD // N_HEAD
    branch = jnp.zeros((TOKENS, D), jnp.float32)
    for group_idx in range(N_HEAD):
        lower = group_idx * group_rows
        part_term = jnp.dot(attended[:, lower:lower + group_rows], w_o[lower:lower + group_rows], preferred_element_type=jnp.float32).astype(jnp.bfloat16)
        branch = branch + lax.optimization_barrier(part_term).astype(jnp.float32)
    mixed_out = tokens_f32 + rms_scale(branch, post_gain)
    return mixed_out.astype(jnp.bfloat16)
```

```python
import functools
import numpy as np
import jax
import jax.numpy as jnp
from jax import lax
from jax.experimental import pallas as pl
from jax.experimental.pallas import tpu as pltpu
from jax.sharding import PartitionSpec as P

D = 5376
HD = 128
WINDOW = 1024
PAGE = 256
NZ, NY, NX = 16, 4, 4
T = 512
OWN = 672
PIECE = 84
NEXT = 128
SPAN = 3 * T + NEXT
SCALE = 168.0 ** (-0.5)
EPS = 1e-06
NEG = -1e30
NSEM = 240
TILE = 256


def rope_tables():
    freq = 10000.0 ** (-2.0 * np.arange(64, dtype=np.float64) / HD)
    inner = np.arange(T, dtype=np.float64)[:, None] * freq[None, :]
    outer = np.arange(NZ * NY, dtype=np.float64)[:, None] * T * freq[None, :]
    sign = np.concatenate([-np.ones(64), np.ones(64)])
    both = lambda a: np.concatenate([a, a], axis=1)
    rows = np.stack([both(np.cos(inner)), both(np.sin(inner)) * sign])
    base = np.stack([both(np.cos(outer)), both(np.sin(outer)) * sign])
    return rows.astype(np.float32), base.astype(np.float32)


def kernel(
    tok_ref, gain_ref, post_ref, wq_ref, wo_ref, rows_ref, base_ref, start_ref, page_ref,
    out_ref,
    xbuf, wa, wb, wob, kbuf, vbuf, qbuf, att, sq1, sq2, acc, wc, woc, oacc, ssem, rsem,
):
    c = lax.axis_index("ctx")
    h = lax.axis_index("head")
    z, y = c // NY, c % NY
    x, k = h // 2, h % 2
    counter = [0]
    pending = []

    def dev(dz=0, dy=0):
        return {"ctx": ((z + dz) % NZ) * NY + (y + dy) % NY, "head": h}

    def dev_c(dc):
        return {"ctx": (c + dc) % (NZ * NY), "head": h}

    def dev_h(hh):
        return {"ctx": c, "head": hh}

    def chan():
        counter[0] += 1
        assert counter[0] <= NSEM
        return counter[0] - 1

    def copy_of(i, src, dst, to):
        return pltpu.make_async_remote_copy(
            src_ref=src, dst_ref=dst, send_sem=ssem.at[i], recv_sem=rsem.at[i],
            device_id=to, device_id_type=pl.DeviceIdType.MESH,
        )

    def send(i, ref, to, src=None, when=None):
        made = copy_of(i, ref if src is None else src, ref, to)
        if when is None:
            made.start()
        else:
            pl.when(when)(made.start)
        pending.append((made, when))

    def recv(i, ref, when=None):
        made = copy_of(i, ref, ref, dev(1))
        if when is None:
            made.wait_recv()
        else:
            pl.when(when)(made.wait_recv)

    peers = [dev(1), dev(-1), dev(0, 1), dev(0, -1), dev(0, 2), dev_c(1), dev_c(-1), dev_c(2), dev_c(-2)]
    peers += [dev_h((h + i) % 8) for i in range(1, 8)]
    barrier = pltpu.get_barrier_semaphore()
    for to in peers:
        pl.semaphore_signal(barrier, inc=1, device_id=to, device_id_type=pl.DeviceIdType.MESH)
    wa[c] = wq_ref[:, 0:256]
    wb[c] = wq_ref[:, 256:512]
    root = z // 2
    mine = (z % 2) * NY + y

    @pl.when(h == root)
    def _():
        wob[mine, h] = wo_ref[...]

    pl.semaphore_wait(barrier, len(peers))

    slot = lambda dz, dy=0: ((z + dz) % NZ) * NY + (y + dy) % NY
    group = lambda dz: pl.ds(((z + dz) % NZ) * NY, NY)

    zp = {s: chan() for s in range(1, 9)}
    zm = {s: chan() for s in range(1, 9)}
    steps = [0, 1, -1, 2, -2, 3, -3, 4, -4, 5, -5, 6, -6, 7, -7, 8]
    yp = {d: chan() for d in steps}
    ym = {d: chan() for d in steps}
    yh0 = {d: chan() for d in steps}
    yh1 = {d: chan() for d in steps}

    def zb_send(s):
        if s < 8:
            send(zp[s], wb.at[slot(1 - s)], dev(1))
            send(zm[s], wb.at[slot(s - 1)], dev(-1))
        else:
            send(zp[s], wb.at[slot(1 - s), :, 0:128], dev(1))
            send(zm[s], wb.at[slot(s - 1), :, 128:256], dev(-1))

    def zb_recv(s):
        if s < 8:
            recv(zp[s], wb.at[slot(-s)])
            recv(zm[s], wb.at[slot(s)])
        else:
            recv(zp[s], wb.at[slot(-s), :, 0:128])
            recv(zm[s], wb.at[slot(s), :, 128:256])

    def yb_send(d):
        send(yp[d], wb.at[slot(d)], dev(0, 1))
        send(ym[d], wb.at[slot(d)], dev(0, -1))

    def yb_relay(d):
        recv(yp[d], wb.at[slot(d, -1)])
        send(yh0[d], wb.at[slot(d, -1), :, 0:128], dev(0, 1))
        recv(ym[d], wb.at[slot(d, 1)])
        send(yh1[d], wb.at[slot(d, 1), :, 128:256], dev(0, -1))

    def yb_finish(d):
        recv(yh0[d], wb.at[slot(d, 2), :, 0:128])
        recv(yh1[d], wb.at[slot(d, 2), :, 128:256])

    ya = [chan() for _ in range(3)]
    zap = {s: chan() for s in range(1, 9)}
    zam = {s: chan() for s in range(1, 9)}
    half_lo = lambda dz: pl.ds(((z + dz) % NZ) * NY, 2)
    half_hi = lambda dz: pl.ds(((z + dz) % NZ) * NY + 2, 2)

    def za_send(s):
        if s < 8:
            send(zap[s], wa.at[group(1 - s)], dev(1))
            send(zam[s], wa.at[group(s - 1)], dev(-1))
        else:
            send(zap[s], wa.at[half_lo(1 - s)], dev(1))
            send(zam[s], wa.at[half_hi(s - 1)], dev(-1))

    def za_recv(s):
        if s < 8:
            recv(zap[s], wa.at[group(-s)])
            recv(zam[s], wa.at[group(s)])
        else:
            recv(zap[s], wa.at[half_lo(-s)])
            recv(zam[s], wa.at[half_hi(s)])

    class Gather:
        def __init__(self, view, lo, hi):
            self.view, self.lo, self.hi = view, lo, hi
            self.i = [chan() for _ in range(9)]

        def at(self, dx, dk=0):
            return ((x + dx) % NX) * 2 + (k + dk) % 2

        def start(self):
            own = self.view(self.at(0))
            send(self.i[0], own, dev_h(self.at(1)))
            send(self.i[1], own, dev_h(self.at(-1)))
            send(self.i[4], own, dev_h(self.at(0, 1)))

        def relay(self):
            other = dev_h(self.at(0, 1))
            recv(self.i[0], self.view(self.at(-1)))
            send(self.i[2], self.lo(self.at(-1)), dev_h(self.at(1)))
            send(self.i[5], self.view(self.at(-1)), other)
            recv(self.i[1], self.view(self.at(1)))
            send(self.i[3], self.hi(self.at(1)), dev_h(self.at(-1)))
            send(self.i[6], self.view(self.at(1)), other)

        def share(self):
            other = dev_h(self.at(0, 1))
            recv(self.i[2], self.lo(self.at(2)))
            send(self.i[7], self.lo(self.at(2)), other)
            recv(self.i[3], self.hi(self.at(2)))
            send(self.i[8], self.hi(self.at(2)), other)

        def finish(self):
            recv(self.i[4], self.view(self.at(0, 1)))
            recv(self.i[5], self.view(self.at(-1, 1)))
            recv(self.i[6], self.view(self.at(1, 1)))
            recv(self.i[7], self.lo(self.at(2, 1)))
            recv(self.i[8], self.hi(self.at(2, 1)))

    def rows_gather(buf, r0, n):
        return Gather(
            lambda s: buf.at[s, r0:r0 + n], lambda s: buf.at[s, r0:r0 + n // 2],
            lambda s: buf.at[s, r0 + n // 2:r0 + n],
        )

    tok_gathers = [rows_gather(xbuf, 0, 256), rows_gather(xbuf, 256, 256)]

    def exchange_start(buf):
        ids = [chan() for _ in range(7)]
        for i in range(7):
            send(ids[i], buf.at[h], dev_h((h + i + 1) % 8))
        return ids

    def exchange_finish(buf, ids):
        for i in range(7):
            recv(ids[i], buf.at[(h - i - 1) % 8])

    r = (z - 2 * h) % NZ
    up = (r >= 2) & (r <= 8)
    turn = jnp.where(r <= 8, r, NZ + 1 - r)
    wo1 = [chan() for _ in range(8)][0]
    wo2u = [[chan() for _ in range(2)] for _ in range(2)]
    wo2d = [[chan() for _ in range(2)] for _ in range(2)]
    wo3 = [[[chan() for _ in range(4)] for _ in range(2)] for _ in range(2)]
    chunk = lambda b, g, dy=0: wob.at[b * NY + (y + dy) % NY, pl.ds(4 * g, 4)]
    chunk_lo = lambda b, g, dy=0: wob.at[b * NY + (y + dy) % NY, pl.ds(4 * g, 2)]
    chunk_hi = lambda b, g, dy=0: wob.at[b * NY + (y + dy) % NY, pl.ds(4 * g + 2, 2)]

    def wo_piece(hh, to):
        return pltpu.make_async_remote_copy(
            src_ref=wo_ref, dst_ref=wob.at[mine, hh], send_sem=ssem.at[wo1],
            recv_sem=rsem.at[wo1 + hh], device_id=dev_h(to), device_id_type=pl.DeviceIdType.MESH,
        )

    def wo_chain(b, g, upward):
        return pltpu.make_async_remote_copy(
            src_ref=chunk(b, g), dst_ref=chunk(b, g),
            send_sem=ssem.at[(wo2u if upward else wo2d)[b][g]], recv_sem=rsem.at[wo2u[b][g]],
            device_id=dev(1 if upward else -1), device_id_type=pl.DeviceIdType.MESH,
        )

    def wo_root():
        @pl.when(r < 2)
        def _():
            for i in range(1, 8):
                wo_piece((h + i) % 8, (h + i) % 8).wait_recv()
        for b in range(2):
            @pl.when(r == b)
            def _():
                for g in range(2):
                    wo_chain(b, g, True).start()
                    wo_chain(b, g, False).start()

    def wo_turn(s):
        for upward in (True, False):
            if s == 1:
                cond, blocks = (r == 1, [0]) if upward else (r == 0, [1])
            else:
                cond, blocks = (turn == s) & (up if upward else jnp.logical_not(up)) & (r >= 2), [0, 1]
            @pl.when(cond)
            def _():
                for b in blocks:
                    for g in range(2):
                        wo_chain(b, g, upward).wait_recv()
                        if s < 8:
                            wo_chain(b, g, upward).start()

    def wo_sent():
        @pl.when(h != root)
        def _():
            wo_piece(h, root).wait_send()
        conds = {
            (0, True): r <= 7, (1, True): (r >= 1) & (r <= 7),
            (0, False): (r == 0) | (r >= 10), (1, False): (r <= 1) | (r >= 10),
        }
        for (b, upward), cond in conds.items():
            @pl.when(cond)
            def _():
                for g in range(2):
                    wo_chain(b, g, upward).wait_send()

    def wo_y_send(b):
        for g in range(2):
            send(wo3[b][g][0], chunk(b, g), dev(0, 1))
            send(wo3[b][g][1], chunk(b, g), dev(0, -1))

    def wo_y_relay(b):
        for g in range(2):
            recv(wo3[b][g][0], chunk(b, g, -1))
            send(wo3[b][g][2], chunk_lo(b, g, -1), dev(0, 1))
            recv(wo3[b][g][1], chunk(b, g, 1))
            send(wo3[b][g][3], chunk_hi(b, g, 1), dev(0, -1))

    def wo_y_finish(b):
        for g in range(2):
            recv(wo3[b][g][2], chunk_lo(b, g, 2))
            recv(wo3[b][g][3], chunk_hi(b, g, 2))

    zb_send(1)
    for dy, i in ((1, 0), (-1, 1), (2, 2)):
        send(ya[i], wa.at[slot(0)], dev(0, dy))
    yb_send(0)

    @pl.when(h != root)
    def _():
        wo_piece(h, root).start()

    part = jnp.zeros((1, T), jnp.float32)
    gain = gain_ref[pl.ds(h, 1), :]
    for j in range(6):
        n = min(128, OWN - 128 * j)
        piece = tok_ref[128 * j:128 * j + n, :].astype(jnp.float32)
        part = part + jnp.sum(piece * piece, axis=0, keepdims=True)
        if n < 128:
            piece = jnp.concatenate([piece, jnp.zeros((128 - n, T), jnp.float32)], axis=0)
        xbuf[h, :, 128 * j:128 * j + 128] = (
            piece.T * gain[:, 128 * j:128 * j + 128]
        ).astype(jnp.bfloat16)
    sq1[h] = jnp.broadcast_to(part, (8, T))
    for gather in tok_gathers:
        gather.start()
    sq1_ids = exchange_start(sq1)
    for dy, i in ((-1, 0), (1, 1), (2, 2)):
        recv(ya[i], wa.at[slot(0, dy)])
    za_send(1)
    wo_root()

    wc[OWN:768, :] = jnp.zeros((768 - OWN, T), jnp.bfloat16)
    for s in range(1, 9):
        zb_recv(s)
        if s < 8:
            zb_send(s + 1)
            yb_send(s)
            yb_send(-s)
        else:
            yb_send(8)
        za_recv(s)
        if s < 8:
            za_send(s + 1)
        wo_turn(s)
        for d in ([0] if s == 1 else [s - 1, 1 - s]):
            yb_relay(d)
        if s == 2:
            tok_gathers[0].relay()
        if s == 4:
            tok_gathers[1].relay()
        if s == 5:
            tok_gathers[0].share()
        if s == 6:
            tok_gathers[1].share()
    yb_relay(8)
    wo_y_send(0)
    for d in steps:
        yb_finish(d)
    for gather in tok_gathers:
        gather.finish()
    exchange_finish(sq1, sq1_ids)

    acc[...] = jnp.zeros_like(acc)

    def project(hh, carry):
        for i in range(8):
            wc[PIECE * i:PIECE * i + PIECE, 0:256] = wa[8 * hh + i]
            wc[PIECE * i:PIECE * i + PIECE, 256:512] = wb[8 * hh + i]
        acc[...] += jnp.dot(xbuf[hh], wc[...], preferred_element_type=jnp.float32)
        return carry

    lax.fori_loop(0, 8, project, 0)
    total = jnp.sum(sq1[...], axis=0)[0:1, :]
    inverse = lax.rsqrt(total / D + EPS)
    inverse = jnp.broadcast_to(inverse, (128, T)).T
    cos_in, sin_in = rows_ref[0], rows_ref[1]
    cos_out, sin_out = base_ref[0, pl.ds(c, 1), :], base_ref[1, pl.ds(c, 1), :]
    cosine = cos_in * cos_out - sin_in * sin_out
    sine = sin_in * cos_out + cos_in * sin_out

    def turned(v):
        v = v * inverse
        return (v * cosine + pltpu.roll(v, 64, 1) * sine).astype(jnp.bfloat16)

    kbuf[2 * T:3 * T, :] = turned(acc[:, 256:384])
    vbuf[2 * T:3 * T, :] = (acc[:, 384:512] * inverse).astype(jnp.bfloat16)
    halo = [chan() for _ in range(6)]
    for i, buf in enumerate((kbuf, vbuf)):
        own = buf.at[2 * T:3 * T]
        send(halo[i], buf.at[T:2 * T], dev_c(1), src=own)
        send(halo[2 + i], buf.at[0:T], dev_c(2), src=own)
        send(halo[4 + i], buf.at[3 * T:SPAN], dev_c(-1), src=buf.at[2 * T:2 * T + NEXT])
    wo_y_send(1)
    wo_y_relay(0)
    qbuf[0] = turned(acc[:, 0:128])
    qbuf[1] = turned(acc[:, 128:256])
    for i, buf in enumerate((kbuf, vbuf)):
        recv(halo[i], buf.at[T:2 * T])
        recv(halo[2 + i], buf.at[0:T])
        recv(halo[4 + i], buf.at[3 * T:SPAN])

    pages = page_ref[...]
    here = jnp.max(jnp.where(pages == c, 1, 0), axis=(0, 1), keepdims=True)
    before = jnp.max(jnp.where(pages == c - 1, 1, 0), axis=(0, 1), keepdims=True)
    first_here = start_ref[c] - c * T
    first_before = start_ref[jnp.maximum(c - 1, 0)] - c * T
    nt = (((1,), (1,)), ((), ()))
    att_gathers = [rows_gather(att, 0, 256), rows_gather(att, 256, 256)]
    for tile in range(2):
        rows = TILE * tile + lax.broadcasted_iota(jnp.int32, (TILE, 1), 0)
        far = 1 << 20
        low = jnp.where(
            (here > 0) & (rows >= first_here) & (rows < first_here + PAGE), first_here,
            jnp.where(
                (before > 0) & (rows >= first_before) & (rows < first_before + PAGE) & (c > 0),
                first_before, far,
            ),
        )

        def head(j, carry):
            q = qbuf[j, TILE * tile:TILE * tile + TILE, :]
            keys = lambda lo, n: kbuf[lo:lo + n, :]
            dots = lambda lo, n: lax.dot_general(q, keys(lo, n), nt, preferred_element_type=jnp.float32)
            cols = lax.broadcasted_iota(jnp.int32, (TILE, T), 1)
            s0 = jnp.where((cols > rows) & (c > 1), dots(0, T), NEG)
            s1 = jnp.where(c > 0, dots(T, T), NEG)
            s2 = jnp.where((cols <= rows) | ((cols >= low) & (cols < low + PAGE)), dots(2 * T, T), NEG)
            cols = T + lax.broadcasted_iota(jnp.int32, (TILE, NEXT), 1)
            s3 = jnp.where((cols >= low) & (cols < low + PAGE), dots(3 * T, NEXT), NEG)
            parts = [s0, s1, s2, s3]
            top = functools.reduce(jnp.maximum, [jnp.max(s, axis=1, keepdims=True) for s in parts])
            weight = [jnp.exp((s - top) * SCALE) for s in parts]
            norm = sum(jnp.sum(w, axis=1, keepdims=True) for w in weight)
            mixed = jnp.zeros((TILE, HD), jnp.float32)
            for w, (lo, n) in zip(weight, ((0, T), (T, T), (2 * T, T), (3 * T, NEXT))):
                mixed += jnp.dot(w.astype(jnp.bfloat16), vbuf[lo:lo + n, :], preferred_element_type=jnp.float32)
            mixed = (mixed / norm).astype(jnp.bfloat16)
            return mixed

        for j in range(2):
            att[h, TILE * tile:TILE * tile + TILE, HD * j:HD * j + HD] = head(j, 0)
        att_gathers[tile].start()
        if tile == 0:
            wo_y_relay(1)
    for gather in att_gathers:
        gather.relay()
    wo_y_finish(0)
    wo_y_finish(1)

    def compact(hh, carry):
        for i in range(8):
            woc[hh, PIECE * i:PIECE * i + PIECE, :] = wob[i, hh]
        return carry

    lax.fori_loop(0, 8, compact, 0)
    for gather in att_gathers:
        gather.share()
    for gather in att_gathers:
        gather.finish()
    oacc[...] = jnp.zeros_like(oacc)

    def project_out(hh, carry):
        oacc[...] += lax.dot_general(woc[hh], att[hh], nt, preferred_element_type=jnp.float32)
        return carry

    lax.fori_loop(0, 8, project_out, 0)
    branch = oacc[...]
    sq2[h] = jnp.broadcast_to(jnp.sum(branch * branch, axis=0, keepdims=True), (8, T))
    sq2_ids = exchange_start(sq2)
    exchange_finish(sq2, sq2_ids)
    total = jnp.sum(sq2[...], axis=0)[0:1, :]
    inverse = lax.rsqrt(total / D + EPS)
    for j in range(4):
        part = oacc[:, 128 * j:128 * j + 128] * inverse[:, 128 * j:128 * j + 128] * post_ref[...]
        out_ref[:, 128 * j:128 * j + 128] = (
            tok_ref[:, 128 * j:128 * j + 128].astype(jnp.float32) + part
        ).astype(jnp.bfloat16)
    for made, when in pending:
        made.wait_send()
    wo_sent()


def per_device(tokens, pre_gain, post_gain, w_qkv, w_o, page_start, page_of):
    rows, base = rope_tables()
    gain = jnp.pad(pre_gain.reshape(8, OWN), ((0, 0), (0, 768 - OWN)))
    own_gain = lax.dynamic_slice_in_dim(post_gain, lax.axis_index("head") * OWN, OWN, 0)
    post = jnp.broadcast_to(own_gain[:, None], (OWN, 128))
    vmem = pl.BlockSpec(memory_space=pltpu.VMEM)
    smem = pl.BlockSpec(memory_space=pltpu.SMEM)
    bf16, f32 = jnp.bfloat16, jnp.float32
    out = pl.pallas_call(
        kernel,
        out_shape=jax.ShapeDtypeStruct((OWN, T), bf16),
        in_specs=[vmem] * 7 + [smem, vmem],
        out_specs=vmem,
        scratch_shapes=[
            pltpu.VMEM((8, T, 768), bf16),
            pltpu.VMEM((64, PIECE, 256), bf16),
            pltpu.VMEM((64, PIECE, 256), bf16),
            pltpu.VMEM((8, 8, PIECE, 256), bf16),
            pltpu.VMEM((SPAN, HD), bf16),
            pltpu.VMEM((SPAN, HD), bf16),
            pltpu.VMEM((2, T, HD), bf16),
            pltpu.VMEM((8, T, 256), bf16),
            pltpu.VMEM((8, 8, T), f32),
            pltpu.VMEM((8, 8, T), f32),
            pltpu.VMEM((T, T), f32),
            pltpu.VMEM((768, T), bf16),
            pltpu.VMEM((8, OWN, 256), bf16),
            pltpu.VMEM((OWN, T), f32),
            pltpu.SemaphoreType.DMA((NSEM,)),
            pltpu.SemaphoreType.DMA((NSEM,)),
        ],
        compiler_params=pltpu.CompilerParams(
            collective_id=0, has_side_effects=True, vmem_limit_bytes=58 * 1024 * 1024
        ),
    )(tokens.T, gain, post, w_qkv, w_o.T, jnp.asarray(rows), jnp.asarray(base), page_start, page_of.reshape(4, 128))
    return out.T


def solution(mesh):
    return jax.shard_map(
        per_device,
        mesh=mesh,
        in_specs=(P("ctx", "head"), P(), P(), P("ctx", "head"), P("head", "ctx"), P(), P("ctx")),
        out_specs=P("ctx", "head"),
        check_vma=False,
    )
```

```python
import functools
import numpy as np
import jax
import jax.numpy as jnp
from jax import lax
from jax.experimental import pallas as pl
from jax.experimental.pallas import tpu as pltpu
from jax.sharding import PartitionSpec as P

D = 5376
HD = 128
WINDOW = 1024
PAGE = 256
NZ, NY, NX = 16, 4, 4
T = 512
OWN = 672
PIECE = 84
NEXT = 128
SPAN = 3 * T + NEXT
SCALE = 168.0 ** (-0.5)
EPS = 1e-06
NEG = -1e30
NSEM = 340
EARLY = 8
TILE = 256


def rope_tables():
    freq = 10000.0 ** (-2.0 * np.arange(64, dtype=np.float64) / HD)
    inner = np.arange(T, dtype=np.float64)[:, None] * freq[None, :]
    outer = np.arange(NZ * NY, dtype=np.float64)[:, None] * T * freq[None, :]
    sign = np.concatenate([-np.ones(64), np.ones(64)])
    both = lambda a: np.concatenate([a, a], axis=1)
    rows = np.stack([both(np.cos(inner)), both(np.sin(inner)) * sign])
    base = np.stack([both(np.cos(outer)), both(np.sin(outer)) * sign])
    return rows.astype(np.float32), base.astype(np.float32)


def kernel(
    tok_ref, gain_ref, wq_ref, wo_ref, rows_ref, base_ref, page_ref, start_ref,
    oacc, inv_ref,
    tok_buf, gain_buf, rows_buf, base_buf, page_buf,
    xbuf, wa, wb, wob, kbuf, vbuf, qbuf, tops, norms, sums, att, sq1, sq2, acc, wc, woc, ssem, rsem, lsem,
):
    c = lax.axis_index("ctx")
    h = lax.axis_index("head")
    z, y = c // NY, c % NY
    x, k = h // 2, h % 2
    counter = [0]
    pending = []

    def dev(dz=0, dy=0):
        return {"ctx": ((z + dz) % NZ) * NY + (y + dy) % NY, "head": h}

    def dev_c(dc):
        return {"ctx": (c + dc) % (NZ * NY), "head": h}

    def dev_h(hh):
        return {"ctx": c, "head": hh}

    def chan():
        counter[0] += 1
        assert counter[0] <= NSEM
        return counter[0] - 1

    def copy_of(i, src, dst, to):
        return pltpu.make_async_remote_copy(
            src_ref=src, dst_ref=dst, send_sem=ssem.at[i], recv_sem=rsem.at[i],
            device_id=to, device_id_type=pl.DeviceIdType.MESH,
        )

    def send(i, ref, to, src=None, when=None):
        made = copy_of(i, ref if src is None else src, ref, to)
        if when is None:
            made.start()
        else:
            pl.when(when)(made.start)
        pending.append((made, when))

    def recv(i, ref, when=None):
        made = copy_of(i, ref, ref, dev(1))
        if when is None:
            made.wait_recv()
        else:
            pl.when(when)(made.wait_recv)

    root, lane = z // 2, (z % 2) * 8 + h
    source_z, source_h = 2 * h + z // 8, z % 8
    moves = (root != h) | (lane != z)
    to_piece = {"ctx": lane * NY + y, "head": root}
    from_piece = {"ctx": source_z * NY + y, "head": source_h}
    peers = [dev(1), dev(-1), dev(0, 1), dev(0, -1), dev(0, 2), dev_c(1), dev_c(-1), dev_c(2), dev_c(-2)]
    peers += [dev_h((h + i) % 8) for i in range(1, 8)]
    barrier = pltpu.get_barrier_semaphore()

    def greet(to):
        pl.semaphore_signal(barrier, inc=1, device_id=to, device_id_type=pl.DeviceIdType.MESH)

    slot = lambda dz, dy=0: ((z + dz) % NZ) * NY + (y + dy) % NY

    def slot_o(dz, dy=0):
        zz, yy = (z + dz) % NZ, (y + dy) % NY
        return ((zz // 8) * NY + yy) * 8 + zz % 8

    fetch = [
        pltpu.make_async_copy(wq_ref.at[:, 256:512], wb.at[c], lsem.at[0]),
        pltpu.make_async_copy(wq_ref.at[:, 0:256], wa.at[c], lsem.at[1]),
        pltpu.make_async_copy(tok_ref, tok_buf, lsem.at[2]),
        pltpu.make_async_copy(gain_ref, gain_buf, lsem.at[3]),
        pltpu.make_async_copy(rows_ref, rows_buf, lsem.at[4]),
        pltpu.make_async_copy(base_ref, base_buf, lsem.at[5]),
        pltpu.make_async_copy(page_ref, page_buf, lsem.at[6]),
    ]
    for f in fetch:
        f.start()
    for to in peers:
        greet(to)

    @pl.when(moves)
    def _():
        greet(to_piece)
        greet(from_piece)

    pl.semaphore_wait(barrier, len(peers) + 2 * jnp.where(moves, 1, 0))
    fetch[0].wait()
    fetch[1].wait()

    steps = [0, 1, -1, 2, -2, 3, -3, 4, -4, 5, -5, 6, -6, 7, -7, 8]

    class ZThenY:
        def __init__(self, buf, slot):
            self.buf, self.slot = buf, slot
            self.zp = {s: chan() for s in range(1, 9)}
            self.zm = {s: chan() for s in range(1, 9)}
            self.yp, self.ym, self.h0, self.h1 = ({d: chan() for d in steps} for _ in range(4))

        def full(self, dz, dy=0):
            return self.buf.at[self.slot(dz, dy)]

        def lo(self, dz, dy=0):
            return self.buf.at[self.slot(dz, dy), :, 0:128]

        def hi(self, dz, dy=0):
            return self.buf.at[self.slot(dz, dy), :, 128:256]

        def z_send(self, s):
            send(self.zp[s], (self.full if s < 8 else self.lo)(1 - s), dev(1))
            send(self.zm[s], (self.full if s < 8 else self.hi)(s - 1), dev(-1))

        def z_recv(self, s):
            recv(self.zp[s], (self.full if s < 8 else self.lo)(-s))
            recv(self.zm[s], (self.full if s < 8 else self.hi)(s))

        def y_send(self, d):
            send(self.yp[d], self.full(d), dev(0, 1))
            send(self.ym[d], self.full(d), dev(0, -1))

        def y_relay(self, d):
            recv(self.yp[d], self.full(d, -1))
            send(self.h0[d], self.lo(d, -1), dev(0, 1))
            recv(self.ym[d], self.full(d, 1))
            send(self.h1[d], self.hi(d, 1), dev(0, -1))

        def y_finish(self, d):
            recv(self.h0[d], self.lo(d, 2))
            recv(self.h1[d], self.hi(d, 2))

    ring_b = ZThenY(wb, slot)
    ring_o = ZThenY(wob, slot_o)

    beside = [0, -1, 1, 2]
    ya = [chan() for _ in range(3)]
    zap = {(s, q): chan() for s in range(1, 9) for q in (beside if s < 8 else beside[:2])}
    zam = {(s, q): chan() for s in range(1, 9) for q in (beside if s < 8 else beside[2:])}

    def za_send(s, q):
        if (s, q) in zap:
            send(zap[s, q], wa.at[slot(1 - s, q)], dev(1))
        if (s, q) in zam:
            send(zam[s, q], wa.at[slot(s - 1, q)], dev(-1))

    def za_recv(s, q):
        if (s, q) in zap:
            recv(zap[s, q], wa.at[slot(-s, q)])
        if (s, q) in zam:
            recv(zam[s, q], wa.at[slot(s, q)])

    class Gather:
        def __init__(self, view, lo, hi):
            self.view, self.lo, self.hi = view, lo, hi
            self.i = [chan() for _ in range(9)]

        def at(self, dx, dk=0):
            return ((x + dx) % NX) * 2 + (k + dk) % 2

        def start(self):
            own = self.view(self.at(0))
            send(self.i[0], own, dev_h(self.at(1)))
            send(self.i[1], own, dev_h(self.at(-1)))
            send(self.i[4], own, dev_h(self.at(0, 1)))

        def relay(self):
            other = dev_h(self.at(0, 1))
            recv(self.i[0], self.view(self.at(-1)))
            send(self.i[2], self.lo(self.at(-1)), dev_h(self.at(1)))
            send(self.i[5], self.view(self.at(-1)), other)
            recv(self.i[1], self.view(self.at(1)))
            send(self.i[3], self.hi(self.at(1)), dev_h(self.at(-1)))
            send(self.i[6], self.view(self.at(1)), other)

        def share(self):
            other = dev_h(self.at(0, 1))
            recv(self.i[2], self.lo(self.at(2)))
            send(self.i[7], self.lo(self.at(2)), other)
            recv(self.i[3], self.hi(self.at(2)))
            send(self.i[8], self.hi(self.at(2)), other)

        def finish(self):
            recv(self.i[4], self.view(self.at(0, 1)))
            recv(self.i[5], self.view(self.at(-1, 1)))
            recv(self.i[6], self.view(self.at(1, 1)))
            recv(self.i[7], self.lo(self.at(2, 1)))
            recv(self.i[8], self.hi(self.at(2, 1)))

    def rows_gather(buf, r0, n):
        return Gather(
            lambda s: buf.at[s, r0:r0 + n], lambda s: buf.at[s, r0:r0 + n // 2],
            lambda s: buf.at[s, r0 + n // 2:r0 + n],
        )

    tok_gathers = [rows_gather(xbuf, 0, 256), rows_gather(xbuf, 256, 256)]

    def exchange_start(buf):
        ids = [chan() for _ in range(7)]
        for i in range(7):
            send(ids[i], buf.at[h], dev_h((h + i + 1) % 8))
        return ids

    def exchange_finish(buf, ids):
        for i in range(7):
            recv(ids[i], buf.at[(h - i - 1) % 8])

    piece_id = chan()
    piece = copy_of(piece_id, wo_ref, wob.at[(((lane // 8) * NY + y) * 8 + lane % 8)], to_piece)
    piece_home = pltpu.make_async_copy(wo_ref, wob.at[slot_o(0)], lsem.at[7])

    ring_b.z_send(1)
    za_send(1, 0)
    for dy, i in ((1, 0), (-1, 1), (2, 2)):
        send(ya[i], wa.at[slot(0)], dev(0, dy))
    ring_b.y_send(0)
    pl.when(moves)(piece.start)
    pl.when(jnp.logical_not(moves))(piece_home.start)

    fetch[2].wait()
    fetch[3].wait()
    part = jnp.zeros((1, T), jnp.float32)
    gain = gain_buf[pl.ds(h, 1), :]
    for j in range(6):
        n = min(128, OWN - 128 * j)
        chunk = tok_buf[128 * j:128 * j + n, :].astype(jnp.float32)
        part = part + jnp.sum(chunk * chunk, axis=0, keepdims=True)
        if n < 128:
            chunk = jnp.concatenate([chunk, jnp.zeros((128 - n, T), jnp.float32)], axis=0)
        xbuf[h, :, 128 * j:128 * j + 128] = (
            chunk.T * gain[:, 128 * j:128 * j + 128]
        ).astype(jnp.bfloat16)
    sq1[h] = jnp.broadcast_to(part, (8, T))
    for gather in tok_gathers:
        gather.start()
    sq1_ids = exchange_start(sq1)
    for dy, i in ((-1, 0), (1, 1), (2, 2)):
        recv(ya[i], wa.at[slot(0, dy)])
        za_send(1, dy)

    @pl.when(moves)
    def _():
        copy_of(piece_id, wo_ref, wob.at[slot_o(0)], to_piece).wait_recv()

    pl.when(jnp.logical_not(moves))(piece_home.wait)
    ring_o.z_send(1)
    if 0 <= EARLY:
        ring_o.y_send(0)
    wc[OWN:768, :] = jnp.zeros((768 - OWN, T), jnp.bfloat16)
    for s in range(1, 9):
        for q in beside:
            za_recv(s, q)
            if s < 8:
                za_send(s + 1, q)
        ring_b.z_recv(s)
        if s < 8:
            ring_b.z_send(s + 1)
        for d in ([s, -s] if s < 8 else [8]):
            ring_b.y_send(d)
        ring_o.z_recv(s)
        if s < 8:
            ring_o.z_send(s + 1)
        for d in ([s, -s] if s < 8 else [8]):
            if abs(d) <= EARLY:
                ring_o.y_send(d)
        for d in ([0] if s == 1 else [s - 1, 1 - s]):
            ring_b.y_relay(d)
        if s == 2:
            tok_gathers[0].relay()
        if s == 4:
            tok_gathers[1].relay()
        if s == 5:
            tok_gathers[0].share()
        if s == 6:
            tok_gathers[1].share()
    ring_b.y_relay(8)
    for gather in tok_gathers:
        gather.finish()
    exchange_finish(sq1, sq1_ids)
    for d in steps:
        ring_b.y_finish(d)

    acc[...] = jnp.zeros_like(acc)

    def project(hh, carry):
        for i in range(8):
            wc[PIECE * i:PIECE * i + PIECE, 0:256] = wa[8 * hh + i]
            wc[PIECE * i:PIECE * i + PIECE, 256:512] = wb[8 * hh + i]
        acc[...] += jnp.dot(xbuf[hh], wc[...], preferred_element_type=jnp.float32)
        return carry

    lax.fori_loop(0, 8, project, 0)
    fetch[4].wait()
    fetch[5].wait()
    fetch[6].wait()
    total = jnp.sum(sq1[...], axis=0)[0:1, :]
    inverse = lax.rsqrt(total / D + EPS)
    inverse = jnp.broadcast_to(inverse, (128, T)).T
    cos_in, sin_in = rows_buf[0], rows_buf[1]
    cos_out, sin_out = base_buf[0, pl.ds(c, 1), :], base_buf[1, pl.ds(c, 1), :]
    cosine = cos_in * cos_out - sin_in * sin_out
    sine = sin_in * cos_out + cos_in * sin_out

    def turned(v):
        v = v * inverse
        return (v * cosine + pltpu.roll(v, 64, 1) * sine).astype(jnp.bfloat16)

    kbuf[2 * T:3 * T, :] = turned(acc[:, 256:384])
    vbuf[2 * T:3 * T, :] = (acc[:, 384:512] * inverse).astype(jnp.bfloat16)
    halo = [chan() for _ in range(6)]
    for i, buf in enumerate((kbuf, vbuf)):
        own = buf.at[2 * T:3 * T]
        send(halo[i], buf.at[T:2 * T], dev_c(1), src=own)
        send(halo[2 + i], buf.at[0:T], dev_c(2), src=own)
        send(halo[4 + i], buf.at[3 * T:SPAN], dev_c(-1), src=buf.at[2 * T:2 * T + NEXT])
    qbuf[0] = turned(acc[:, 0:128])
    qbuf[1] = turned(acc[:, 128:256])
    for d in steps:
        if abs(d) > EARLY:
            ring_o.y_send(d)

    pages = page_buf[...]
    here = jnp.max(jnp.where(pages == c, 1, 0), axis=(0, 1), keepdims=True)
    before = jnp.max(jnp.where(pages == c - 1, 1, 0), axis=(0, 1), keepdims=True)
    first_here = start_ref[c] - c * T
    first_before = start_ref[jnp.maximum(c - 1, 0)] - c * T
    nt = (((1,), (1,)), ((), ()))
    att_gathers = [rows_gather(att, 0, 256), rows_gather(att, 256, 256)]
    tiles = [pl.ds(TILE * tile, TILE) for tile in range(T // TILE)]
    row_ids = [TILE * tile + lax.broadcasted_iota(jnp.int32, (TILE, 1), 0) for tile in range(T // TILE)]
    lows = [
        jnp.where(
            (here > 0) & (rows >= first_here) & (rows < first_here + PAGE), first_here,
            jnp.where(
                (before > 0) & (rows >= first_before) & (rows < first_before + PAGE) & (c > 0),
                first_before, 1 << 20,
            ),
        )
        for rows in row_ids
    ]

    def attend(tile, j, spans, first=False, last=False):
        q = qbuf[j, tiles[tile], :]
        rows, low = row_ids[tile], lows[tile]
        parts = []
        for lo, n in spans:
            dots = lax.dot_general(q, kbuf[lo:lo + n, :], nt, preferred_element_type=jnp.float32)
            cols = lo - 2 * T + lax.broadcasted_iota(jnp.int32, (TILE, n), 1)
            if lo < T:
                keep = (cols > rows - WINDOW) & (c > 1)
            elif lo < 2 * T:
                keep = c > 0
            else:
                keep = (cols >= low) & (cols < low + PAGE)
                if lo < 3 * T:
                    keep = keep | (cols <= rows)
            parts.append(jnp.where(keep, dots, NEG))
        top = functools.reduce(jnp.maximum, [jnp.max(s, axis=1, keepdims=True) for s in parts])
        if not first:
            old = tops[j, tiles[tile], 0:1]
            top = jnp.maximum(old, top)
        weight = [jnp.exp((s - top) * SCALE) for s in parts]
        norm = sum(jnp.sum(w, axis=1, keepdims=True) for w in weight)
        mixed = sum(
            jnp.dot(w.astype(jnp.bfloat16), vbuf[lo:lo + n, :], preferred_element_type=jnp.float32)
            for w, (lo, n) in zip(weight, spans)
        )
        if not first:
            fade = jnp.exp((old - top) * SCALE)
            norm = norm + fade * norms[j, tiles[tile], 0:1]
            mixed = mixed + fade * sums[j, tiles[tile], :]
        if last:
            att[h, tiles[tile], HD * j:HD * j + HD] = (mixed / norm).astype(jnp.bfloat16)
        else:
            tops[j, tiles[tile], :] = jnp.broadcast_to(top, (TILE, HD))
            norms[j, tiles[tile], :] = jnp.broadcast_to(norm, (TILE, HD))
            sums[j, tiles[tile], :] = mixed

    def halo_recv(pair, lo, n):
        recv(halo[pair], kbuf.at[lo:lo + n])
        recv(halo[pair + 1], vbuf.at[lo:lo + n])

    for tile in range(T // TILE):
        for j in range(2):
            attend(tile, j, [(2 * T, T)], first=True)
    halo_recv(0, T, T)
    for tile in range(T // TILE):
        for j in range(2):
            attend(tile, j, [(T, T)])
    for d in steps:
        if abs(d) <= EARLY:
            ring_o.y_relay(d)
    halo_recv(4, 3 * T, NEXT)
    halo_recv(2, 0, T)
    for tile in range(T // TILE):
        for j in range(2):
            attend(tile, j, [(TILE * tile, T - TILE * tile), (3 * T, NEXT)], last=True)
        att_gathers[tile].start()
    for d in steps:
        if abs(d) > EARLY:
            ring_o.y_relay(d)
    for gather in att_gathers:
        gather.relay()
    for d in steps:
        ring_o.y_finish(d)

    def compact(hh, carry):
        for i in range(8):
            woc[hh, PIECE * i:PIECE * i + PIECE, :] = wob[8 * i + hh]
        return carry

    lax.fori_loop(0, 8, compact, 0)
    for gather in att_gathers:
        gather.share()
    for gather in att_gathers:
        gather.finish()
    oacc[...] = jnp.zeros_like(oacc)

    def project_out(hh, carry):
        oacc[...] += lax.dot_general(woc[hh], att[hh], nt, preferred_element_type=jnp.float32)
        return carry

    lax.fori_loop(0, 8, project_out, 0)
    branch = oacc[...]
    sq2[h] = jnp.broadcast_to(jnp.sum(branch * branch, axis=0, keepdims=True), (8, T))
    sq2_ids = exchange_start(sq2)
    exchange_finish(sq2, sq2_ids)
    total = jnp.sum(sq2[...], axis=0)[0:1, :]
    inverse = lax.rsqrt(total / D + EPS)
    inv_ref[...] = jnp.broadcast_to(inverse, (8, T))
    for made, when in pending:
        made.wait_send()
    pl.when(moves)(piece.wait_send)


def per_device(tokens, pre_gain, post_gain, w_qkv, w_o, page_start, page_of):
    rows, base = rope_tables()
    gain = jnp.pad(pre_gain.reshape(8, OWN), ((0, 0), (0, 768 - OWN)))
    vmem = pl.BlockSpec(memory_space=pltpu.VMEM)
    smem = pl.BlockSpec(memory_space=pltpu.SMEM)
    anywhere = pl.BlockSpec(memory_space=pl.ANY)
    bf16, f32 = jnp.bfloat16, jnp.float32
    branch, inverse = pl.pallas_call(
        kernel,
        out_shape=(jax.ShapeDtypeStruct((OWN, T), f32), jax.ShapeDtypeStruct((8, T), f32)),
        in_specs=[anywhere] * 7 + [smem],
        out_specs=(vmem, vmem),
        scratch_shapes=[
            pltpu.VMEM((OWN, T), bf16),
            pltpu.VMEM((8, 768), f32),
            pltpu.VMEM((2, T, HD), f32),
            pltpu.VMEM((2, 64, HD), f32),
            pltpu.VMEM((4, 128), jnp.int32),
            pltpu.VMEM((8, T, 768), bf16),
            pltpu.VMEM((64, PIECE, 256), bf16),
            pltpu.VMEM((64, PIECE, 256), bf16),
            pltpu.VMEM((64, PIECE, 256), bf16),
            pltpu.VMEM((SPAN, HD), bf16),
            pltpu.VMEM((SPAN, HD), bf16),
            pltpu.VMEM((2, T, HD), bf16),
            pltpu.VMEM((2, T, HD), f32),
            pltpu.VMEM((2, T, HD), f32),
            pltpu.VMEM((2, T, HD), f32),
            pltpu.VMEM((8, T, 256), bf16),
            pltpu.VMEM((8, 8, T), f32),
            pltpu.VMEM((8, 8, T), f32),
            pltpu.VMEM((T, T), f32),
            pltpu.VMEM((768, T), bf16),
            pltpu.VMEM((8, OWN, 256), bf16),
            pltpu.SemaphoreType.DMA((NSEM,)),
            pltpu.SemaphoreType.DMA((NSEM,)),
            pltpu.SemaphoreType.DMA((8,)),
        ],
        compiler_params=pltpu.CompilerParams(
            collective_id=0, has_side_effects=True, vmem_limit_bytes=58 * 1024 * 1024
        ),
    )(
        tokens.T, gain, w_qkv, w_o.T, jnp.asarray(rows), jnp.asarray(base),
        page_of.reshape(4, 128), page_start,
    )
    own_gain = lax.dynamic_slice_in_dim(post_gain, lax.axis_index("head") * OWN, OWN, 0)
    return (tokens.T.astype(f32) + branch * inverse[0:1, :] * own_gain[:, None]).astype(bf16).T


def solution(mesh):
    return jax.shard_map(
        per_device,
        mesh=mesh,
        in_specs=(P("ctx", "head"), P(), P(), P("ctx", "head"), P("head", "ctx"), P(), P("ctx")),
        out_specs=P("ctx", "head"),
        check_vma=False,
    )
```

```python
import functools
import numpy as np
import jax
import jax.numpy as jnp
from jax import lax
from jax.experimental import pallas as pl
from jax.experimental.pallas import tpu as pltpu
from jax.sharding import PartitionSpec as P

D = 5376
HD = 128
WINDOW = 1024
PAGE = 256
NZ, NY, NX = 16, 4, 4
T = 512
OWN = 672
PIECE = 84
NEXT = 128
SPAN = 3 * T + NEXT
SCALE = 168.0 ** (-0.5)
EPS = 1e-06
NEG = -1e30
NSEM = 298
EARLY = 8
LAG_A, LAG_B, LAG_O, LAG_R, LAG_LAST = 1, 2, 0, 3, 0
TILE = 256


def rope_tables():
    freq = 10000.0 ** (-2.0 * np.arange(64, dtype=np.float64) / HD)
    inner = np.arange(T, dtype=np.float64)[:, None] * freq[None, :]
    outer = np.arange(NZ * NY, dtype=np.float64)[:, None] * T * freq[None, :]
    sign = np.concatenate([-np.ones(64), np.ones(64)])
    both = lambda a: np.concatenate([a, a], axis=1)
    rows = np.stack([both(np.cos(inner)), both(np.sin(inner)) * sign])
    base = np.stack([both(np.cos(outer)), both(np.sin(outer)) * sign])
    return rows.astype(np.float32), base.astype(np.float32)


def kernel(
    tok_ref, pre_ref, post_ref, wq_ref, wo_ref, rows_ref, base_ref, page_ref, start_ref,
    out_ref,
    tok_buf, gain_buf, rows_buf, base_buf, page_buf,
    xbuf, wa, wb, wob, kbuf, vbuf, qbuf, tops, norms, sums, att, sq1, sq2, acc, wc, woc, oacc, ssem, rsem, lsem,
):
    c = lax.axis_index("ctx")
    h = lax.axis_index("head")
    z, y = c // NY, c % NY
    x, k = h // 2, h % 2
    counter = [0]
    pending = []

    def dev(dz=0, dy=0):
        return {"ctx": ((z + dz) % NZ) * NY + (y + dy) % NY, "head": h}

    def dev_c(dc):
        return {"ctx": (c + dc) % (NZ * NY), "head": h}

    def dev_h(hh):
        return {"ctx": c, "head": hh}

    def chan():
        counter[0] += 1
        assert counter[0] <= NSEM
        return counter[0] - 1

    def copy_of(i, src, dst, to):
        return pltpu.make_async_remote_copy(
            src_ref=src, dst_ref=dst, send_sem=ssem.at[i], recv_sem=rsem.at[i],
            device_id=to, device_id_type=pl.DeviceIdType.MESH,
        )

    def send(i, ref, to, src=None, when=None):
        made = copy_of(i, ref if src is None else src, ref, to)
        if when is None:
            made.start()
        else:
            pl.when(when)(made.start)
        pending.append((made, when))

    def recv(i, ref, when=None):
        made = copy_of(i, ref, ref, dev(1))
        if when is None:
            made.wait_recv()
        else:
            pl.when(when)(made.wait_recv)

    root, lane = z // 2, (z % 2) * 8 + h
    source_z, source_h = 2 * h + z // 8, z % 8
    moves = (root != h) | (lane != z)
    to_piece = {"ctx": lane * NY + y, "head": root}
    from_piece = {"ctx": source_z * NY + y, "head": source_h}
    peers = [dev(1), dev(-1), dev(0, 1), dev(0, -1), dev(0, 2), dev_c(1), dev_c(-1), dev_c(2), dev_c(-2)]
    peers += [dev_h((h + i) % 8) for i in range(1, 8)]
    barrier = pltpu.get_barrier_semaphore()

    def greet(to):
        pl.semaphore_signal(barrier, inc=1, device_id=to, device_id_type=pl.DeviceIdType.MESH)

    slot = lambda dz, dy=0: ((z + dz) % NZ) * NY + (y + dy) % NY

    def slot_o(dz, dy=0):
        zz, yy = (z + dz) % NZ, (y + dy) % NY
        return ((zz // 8) * NY + yy) * 8 + zz % 8

    fetch = [
        pltpu.make_async_copy(wq_ref.at[:, 256:512], wb.at[c], lsem.at[0]),
        pltpu.make_async_copy(wq_ref.at[:, 0:256], wa.at[c], lsem.at[1]),
        pltpu.make_async_copy(tok_ref, tok_buf, lsem.at[2]),
        pltpu.make_async_copy(pre_ref, gain_buf.at[0, 0:42], lsem.at[3]),
        pltpu.make_async_copy(rows_ref, rows_buf, lsem.at[4]),
        pltpu.make_async_copy(base_ref, base_buf, lsem.at[5]),
        pltpu.make_async_copy(page_ref, page_buf, lsem.at[6]),
        pltpu.make_async_copy(post_ref, gain_buf.at[1, 0:42], lsem.at[8]),
    ]
    for f in fetch:
        f.start()
    for to in peers:
        greet(to)

    @pl.when(moves)
    def _():
        greet(to_piece)
        greet(from_piece)

    pl.semaphore_wait(barrier, len(peers) + 2 * jnp.where(moves, 1, 0))
    fetch[0].wait()
    fetch[1].wait()

    steps = [0, 1, -1, 2, -2, 3, -3, 4, -4, 5, -5, 6, -6, 7, -7, 8]

    class ZThenY:
        def __init__(self, buf, slot):
            self.buf, self.slot = buf, slot
            self.zp = {s: chan() for s in range(1, 9)}
            self.zm = {s: chan() for s in range(1, 9)}
            self.yp, self.ym, self.h0, self.h1 = ({d: chan() for d in steps} for _ in range(4))

        def full(self, dz, dy=0):
            return self.buf.at[self.slot(dz, dy)]

        def lo(self, dz, dy=0):
            return self.buf.at[self.slot(dz, dy), :, 0:128]

        def hi(self, dz, dy=0):
            return self.buf.at[self.slot(dz, dy), :, 128:256]

        def z_send(self, s):
            send(self.zp[s], (self.full if s < 8 else self.lo)(1 - s), dev(1))
            send(self.zm[s], (self.full if s < 8 else self.hi)(s - 1), dev(-1))

        def z_recv(self, s):
            recv(self.zp[s], (self.full if s < 8 else self.lo)(-s))
            recv(self.zm[s], (self.full if s < 8 else self.hi)(s))

        def y_send(self, d):
            send(self.yp[d], self.full(d), dev(0, 1))
            send(self.ym[d], self.full(d), dev(0, -1))

        def y_relay(self, d):
            recv(self.yp[d], self.full(d, -1))
            send(self.h0[d], self.lo(d, -1), dev(0, 1))
            recv(self.ym[d], self.full(d, 1))
            send(self.h1[d], self.hi(d, 1), dev(0, -1))

        def y_finish(self, d):
            recv(self.h0[d], self.lo(d, 2))
            recv(self.h1[d], self.hi(d, 2))

    ring_b = ZThenY(wb, slot)
    ring_o = ZThenY(wob, slot_o)

    beside = [0, -1, 1, 2]
    ya = [chan() for _ in range(3)]
    zap = {(s, q): chan() for s in range(1, 9) for q in (beside if s < 8 else beside[:2])}
    zam = {(s, q): chan() for s in range(1, 9) for q in (beside if s < 8 else beside[2:])}

    def za_send(s, q):
        if (s, q) in zap:
            send(zap[s, q], wa.at[slot(1 - s, q)], dev(1))
        if (s, q) in zam:
            send(zam[s, q], wa.at[slot(s - 1, q)], dev(-1))

    def za_recv(s, q):
        if (s, q) in zap:
            recv(zap[s, q], wa.at[slot(-s, q)])
        if (s, q) in zam:
            recv(zam[s, q], wa.at[slot(s, q)])

    class Gather:
        def __init__(self, view, lo, hi):
            self.view, self.lo, self.hi = view, lo, hi
            self.i = [chan() for _ in range(9)]

        def at(self, dx, dk=0):
            return ((x + dx) % NX) * 2 + (k + dk) % 2

        def start(self):
            own = self.view(self.at(0))
            send(self.i[0], own, dev_h(self.at(1)))
            send(self.i[1], own, dev_h(self.at(-1)))
            send(self.i[4], own, dev_h(self.at(0, 1)))

        def relay(self):
            other = dev_h(self.at(0, 1))
            recv(self.i[0], self.view(self.at(-1)))
            send(self.i[2], self.lo(self.at(-1)), dev_h(self.at(1)))
            send(self.i[5], self.view(self.at(-1)), other)
            recv(self.i[1], self.view(self.at(1)))
            send(self.i[3], self.hi(self.at(1)), dev_h(self.at(-1)))
            send(self.i[6], self.view(self.at(1)), other)

        def share(self):
            other = dev_h(self.at(0, 1))
            recv(self.i[2], self.lo(self.at(2)))
            send(self.i[7], self.lo(self.at(2)), other)
            recv(self.i[3], self.hi(self.at(2)))
            send(self.i[8], self.hi(self.at(2)), other)

        def finish(self):
            recv(self.i[4], self.view(self.at(0, 1)))
            recv(self.i[5], self.view(self.at(-1, 1)))
            recv(self.i[6], self.view(self.at(1, 1)))
            recv(self.i[7], self.lo(self.at(2, 1)))
            recv(self.i[8], self.hi(self.at(2, 1)))

    class DirectGather(Gather):
        def start(self):
            own = self.view(self.at(0))
            for i, dx in ((0, 1), (1, -1), (2, 2)):
                send(self.i[i], own, dev_h(self.at(dx)))
            send(self.i[3], own, dev_h(self.at(0, 1)))

        def relay(self):
            for i, dx in ((0, -1), (1, 1), (2, 2)):
                recv(self.i[i], self.view(self.at(dx)))
                send(self.i[4 + i], self.view(self.at(dx)), dev_h(self.at(0, 1)))

        def finish(self):
            recv(self.i[3], self.view(self.at(0, 1)))
            for i, dx in ((4, -1), (5, 1), (6, 2)):
                recv(self.i[i], self.view(self.at(dx, 1)))

    def direct_gather(tile, j):
        rows, cols = slice(TILE * tile, TILE * tile + TILE), slice(HD * j, HD * j + HD)
        if tile == 1:
            return DirectGather(lambda s: att.at[s, rows, cols], None, None)
        low, high = slice(0, 128), slice(128, 256)
        return Gather(lambda s: att.at[s, rows, cols], lambda s: att.at[s, low, cols], lambda s: att.at[s, high, cols])

    def rows_gather(buf, r0, n):
        return Gather(
            lambda s: buf.at[s, r0:r0 + n], lambda s: buf.at[s, r0:r0 + n // 2],
            lambda s: buf.at[s, r0 + n // 2:r0 + n],
        )

    tok_gathers = [rows_gather(xbuf, 0, 256), rows_gather(xbuf, 256, 256)]

    def exchange_start(buf):
        ids = [chan() for _ in range(7)]
        for i in range(7):
            send(ids[i], buf.at[h], dev_h((h + i + 1) % 8))
        return ids

    def exchange_finish(buf, ids):
        for i in range(7):
            recv(ids[i], buf.at[(h - i - 1) % 8])

    piece_id = chan()
    piece = copy_of(piece_id, wo_ref, wob.at[(((lane // 8) * NY + y) * 8 + lane % 8)], to_piece)
    piece_home = pltpu.make_async_copy(wo_ref, wob.at[slot_o(0)], lsem.at[7])

    ring_b.z_send(1)
    za_send(1, 0)
    for dy, i in ((1, 0), (-1, 1), (2, 2)):
        send(ya[i], wa.at[slot(0)], dev(0, dy))
    ring_b.y_send(0)
    pl.when(moves)(piece.start)
    pl.when(jnp.logical_not(moves))(piece_home.start)

    fetch[2].wait()
    fetch[3].wait()
    part = jnp.zeros((1, T), jnp.float32)
    first, shift = (h * OWN) // 128, (h * OWN) % 128
    lanes = lax.broadcasted_iota(jnp.int32, (1, 128), 1)

    def own_gain(which, j):
        back = (128 - shift) % 128
        a = pltpu.roll(gain_buf[which, pl.ds(first + j, 1), :], back, 1)
        b = pltpu.roll(gain_buf[which, pl.ds(first + j + 1, 1), :], back, 1)
        return jnp.where(lanes < OWN - 128 * j, jnp.where(lanes < 128 - shift, a, b), 0.0)

    for j in range(6):
        n = min(128, OWN - 128 * j)
        chunk = tok_buf[128 * j:128 * j + n, :].astype(jnp.float32)
        part = part + jnp.sum(chunk * chunk, axis=0, keepdims=True)
        if n < 128:
            chunk = jnp.concatenate([chunk, jnp.zeros((128 - n, T), jnp.float32)], axis=0)
        xbuf[h, :, 128 * j:128 * j + 128] = (
            chunk.T * own_gain(0, j)
        ).astype(jnp.bfloat16)
    sq1[h] = jnp.broadcast_to(part, (8, T))
    for gather in tok_gathers:
        gather.start()
    sq1_ids = exchange_start(sq1)
    for dy, i in ((-1, 0), (1, 1), (2, 2)):
        recv(ya[i], wa.at[slot(0, dy)])
        za_send(1, dy)

    @pl.when(moves)
    def _():
        copy_of(piece_id, wo_ref, wob.at[slot_o(0)], to_piece).wait_recv()

    pl.when(jnp.logical_not(moves))(piece_home.wait)
    ring_o.z_send(1)
    if 0 <= EARLY:
        ring_o.y_send(0)
    wc[OWN:768, :] = jnp.zeros((768 - OWN, 256), jnp.bfloat16)
    both = lambda s: [s, -s] if 0 < s < 8 else [s] if s in (0, 8) else []
    for i in range(1, 9 + LAG_LAST):
        if i <= 8:
            ring_b.z_recv(i)
            if i < 8:
                ring_b.z_send(i + 1)
            for d in both(i):
                ring_b.y_send(d)
        s = i - LAG_A
        if 1 <= s <= 8:
            for q in beside:
                za_recv(s, q)
                if s < 8:
                    za_send(s + 1, q)
        for d in both(i - LAG_B):
            ring_b.y_relay(d)
        s = i - LAG_O
        if 1 <= s <= 8:
            ring_o.z_recv(s)
            if s < 8:
                ring_o.z_send(s + 1)
            for d in both(s):
                if abs(d) <= EARLY:
                    ring_o.y_send(d)
        s = i - LAG_R
        for d in both(s):
            if abs(d) <= EARLY and LAG_R:
                ring_o.y_relay(d)
        if i == 2:
            tok_gathers[0].relay()
        if i == 4:
            tok_gathers[1].relay()
        if i == 5:
            tok_gathers[0].share()
        if i == 6:
            tok_gathers[1].share()
    for s in range(9 + LAG_LAST - LAG_O, 9):
        ring_o.z_recv(s)
        if s < 8:
            ring_o.z_send(s + 1)
        for d in both(s):
            if abs(d) <= EARLY:
                ring_o.y_send(d)
    late_o = [d for d in steps if not LAG_R or abs(d) > EARLY or abs(d) > 8 + LAG_LAST - LAG_R]
    for d in steps:
        if abs(d) > 8 + LAG_LAST - LAG_B:
            ring_b.y_relay(d)
    for gather in tok_gathers:
        gather.finish()
    exchange_finish(sq1, sq1_ids)
    for d in steps:
        ring_b.y_finish(d)

    def project(w, acc):
        def body(hh, carry):
            for i in range(8):
                wc[PIECE * i:PIECE * i + PIECE, :] = w[8 * hh + i]
            part = jnp.dot(xbuf[hh], wc[...], preferred_element_type=jnp.float32)
            acc[...] = acc[...] + part
            return carry

        acc[...] = jnp.zeros_like(acc)
        lax.fori_loop(0, 8, body, 0)

    for f in fetch[4:]:
        f.wait()
    total = jnp.sum(sq1[...], axis=0)[0:1, :]
    inverse = lax.rsqrt(total / D + EPS)
    inverse = jnp.broadcast_to(inverse, (128, T)).T
    cos_in, sin_in = rows_buf[0], rows_buf[1]
    cos_out, sin_out = base_buf[0, pl.ds(c, 1), :], base_buf[1, pl.ds(c, 1), :]
    rows_buf[0], rows_buf[1] = cos_in * cos_out - sin_in * sin_out, sin_in * cos_out + cos_in * sin_out

    def turned(v):
        v = v * inverse
        return (v * rows_buf[0] + pltpu.roll(v, 64, 1) * rows_buf[1]).astype(jnp.bfloat16)

    project(wb, acc)
    kbuf[2 * T:3 * T, :] = turned(acc[:, 0:128])
    vbuf[2 * T:3 * T, :] = (acc[:, 128:256] * inverse).astype(jnp.bfloat16)
    halo = [chan() for _ in range(6)]
    for n, lo, size, dc in ((0, T, T, 1), (4, 3 * T, NEXT, -1), (2, 0, T, 2)):
        for i, buf in enumerate((kbuf, vbuf)):
            send(halo[n + i], buf.at[lo:lo + size], dev_c(dc), src=buf.at[2 * T:2 * T + size])
    for s in range(9 + LAG_LAST - LAG_A, 9):
        for q in beside:
            za_recv(s, q)
            if s < 8:
                za_send(s + 1, q)
    project(wa, acc)
    qbuf[0] = turned(acc[:, 0:128])
    qbuf[1] = turned(acc[:, 128:256])
    for d in steps:
        if abs(d) > EARLY:
            ring_o.y_send(d)

    pages = page_buf[...]
    here = jnp.max(jnp.where(pages == c, 1, 0), axis=(0, 1), keepdims=True)
    before = jnp.max(jnp.where(pages == c - 1, 1, 0), axis=(0, 1), keepdims=True)
    first_here = start_ref[c] - c * T
    first_before = start_ref[jnp.maximum(c - 1, 0)] - c * T
    nt = (((1,), (1,)), ((), ()))
    att_gathers = [[direct_gather(tile, j) for j in range(2)] for tile in range(T // TILE)]
    tiles = [pl.ds(TILE * tile, TILE) for tile in range(T // TILE)]
    row_ids = [TILE * tile + lax.broadcasted_iota(jnp.int32, (TILE, 1), 0) for tile in range(T // TILE)]
    lows = [
        jnp.where(
            (here > 0) & (rows >= first_here) & (rows < first_here + PAGE), first_here,
            jnp.where(
                (before > 0) & (rows >= first_before) & (rows < first_before + PAGE) & (c > 0),
                first_before, 1 << 20,
            ),
        )
        for rows in row_ids
    ]

    def attend(tile, j, spans, first=False, last=False):
        q = qbuf[j, tiles[tile], :]
        rows, low = row_ids[tile], lows[tile]
        parts = []
        for lo, n in spans:
            dots = lax.dot_general(q, kbuf[lo:lo + n, :], nt, preferred_element_type=jnp.float32)
            cols = lo - 2 * T + lax.broadcasted_iota(jnp.int32, (TILE, n), 1)
            if lo < T:
                keep = (cols > rows - WINDOW) & (c > 1)
            elif lo < 2 * T:
                keep = c > 0
            else:
                keep = (cols >= low) & (cols < low + PAGE)
                if lo < 3 * T:
                    keep = keep | (cols <= rows)
            parts.append(jnp.where(keep, dots, NEG))
        top = functools.reduce(jnp.maximum, [jnp.max(s, axis=1, keepdims=True) for s in parts])
        if not first:
            old = tops[j, tiles[tile], 0:1]
            top = jnp.maximum(old, top)
        weight = [jnp.exp((s - top) * SCALE) for s in parts]
        norm = sum(jnp.sum(w, axis=1, keepdims=True) for w in weight)
        mixed = sum(
            jnp.dot(w.astype(jnp.bfloat16), vbuf[lo:lo + n, :], preferred_element_type=jnp.float32)
            for w, (lo, n) in zip(weight, spans)
        )
        if not first:
            fade = jnp.exp((old - top) * SCALE)
            norm = norm + fade * norms[j, tiles[tile], 0:1]
            mixed = mixed + fade * sums[j, tiles[tile], :]
        if last:
            att[h, tiles[tile], HD * j:HD * j + HD] = (mixed / norm).astype(jnp.bfloat16)
        else:
            tops[j, tiles[tile], :] = jnp.broadcast_to(top, (TILE, HD))
            norms[j, tiles[tile], :] = jnp.broadcast_to(norm, (TILE, HD))
            sums[j, tiles[tile], :] = mixed

    def halo_recv(pair, lo, n):
        recv(halo[pair], kbuf.at[lo:lo + n])
        recv(halo[pair + 1], vbuf.at[lo:lo + n])

    for tile in range(T // TILE):
        for j in range(2):
            attend(tile, j, [(2 * T, T)], first=True)
    halo_recv(0, T, T)
    for tile in range(T // TILE):
        for j in range(2):
            attend(tile, j, [(T, T)])
    for d in late_o:
        if abs(d) <= EARLY:
            ring_o.y_relay(d)
    halo_recv(4, 3 * T, NEXT)
    halo_recv(2, 0, T)
    for tile in range(T // TILE):
        for j in range(2):
            attend(tile, j, [(TILE * tile, T - TILE * tile), (3 * T, NEXT)], last=True)
            att_gathers[tile][j].start()
            if tile == 1 and j == 0:
                for g in att_gathers[0]:
                    g.relay()
    for d in late_o:
        if abs(d) > EARLY:
            ring_o.y_relay(d)
    for d in steps:
        ring_o.y_finish(d)

    def compact(hh, carry):
        for i in range(8):
            woc[hh, PIECE * i:PIECE * i + PIECE, :] = wob[8 * i + hh]
        return carry

    lax.fori_loop(0, 8, compact, 0)
    for g in att_gathers[0]:
        g.share()
    for g in att_gathers[0]:
        g.finish()
    for g in att_gathers[1]:
        g.relay()
    squares = []
    for tile in range(T // TILE):
        if tile == 1:
            for g in att_gathers[1]:
                g.finish()
        cols = slice(TILE * tile, TILE * tile + TILE)

        def project_out(hh, carry):
            part = lax.dot_general(woc[hh], att[hh, tiles[tile], :], nt, preferred_element_type=jnp.float32)
            oacc[:, cols] = oacc[:, cols] + part
            return carry

        oacc[:, cols] = jnp.zeros((OWN, TILE), jnp.float32)
        lax.fori_loop(0, 8, project_out, 0)
        branch = oacc[:, cols]
        sq2[h, :, cols] = jnp.broadcast_to(jnp.sum(branch * branch, axis=0, keepdims=True), (8, TILE))
    sq2_ids = exchange_start(sq2)
    for j in range(6):
        n = min(128, OWN - 128 * j)
        spread = jnp.broadcast_to(own_gain(1, j), (128, 128)).T
        for i in range(4):
            cut = (slice(128 * j, 128 * j + n), slice(128 * i, 128 * i + 128))
            oacc[cut] = oacc[cut] * spread[0:n]
    exchange_finish(sq2, sq2_ids)
    total = jnp.sum(sq2[...], axis=0)[0:1, :]
    inverse = lax.rsqrt(total / D + EPS)
    out_ref[...] = (tok_buf[...].astype(jnp.float32) + oacc[...] * inverse).astype(jnp.bfloat16)
    for made, when in pending:
        made.wait_send()
    pl.when(moves)(piece.wait_send)


def per_device(tokens, pre_gain, post_gain, w_qkv, w_o, page_start, page_of):
    rows, base = rope_tables()
    vmem = pl.BlockSpec(memory_space=pltpu.VMEM)
    smem = pl.BlockSpec(memory_space=pltpu.SMEM)
    anywhere = pl.BlockSpec(memory_space=pl.ANY)
    bf16, f32 = jnp.bfloat16, jnp.float32
    out = pl.pallas_call(
        kernel,
        out_shape=jax.ShapeDtypeStruct((OWN, T), bf16),
        in_specs=[anywhere] * 8 + [smem],
        out_specs=vmem,
        scratch_shapes=[
            pltpu.VMEM((OWN, T), bf16),
            pltpu.VMEM((2, 48, 128), f32),
            pltpu.VMEM((2, T, HD), f32),
            pltpu.VMEM((2, 64, HD), f32),
            pltpu.VMEM((4, 128), jnp.int32),
            pltpu.VMEM((8, T, 768), bf16),
            pltpu.VMEM((64, PIECE, 256), bf16),
            pltpu.VMEM((64, PIECE, 256), bf16),
            pltpu.VMEM((64, PIECE, 256), bf16),
            pltpu.VMEM((SPAN, HD), bf16),
            pltpu.VMEM((SPAN, HD), bf16),
            pltpu.VMEM((2, T, HD), bf16),
            pltpu.VMEM((2, T, HD), f32),
            pltpu.VMEM((2, T, HD), f32),
            pltpu.VMEM((2, T, HD), f32),
            pltpu.VMEM((8, T, 256), bf16),
            pltpu.VMEM((8, 8, T), f32),
            pltpu.VMEM((8, 8, T), f32),
            pltpu.VMEM((T, 256), f32),
            pltpu.VMEM((768, 256), bf16),
            pltpu.VMEM((8, OWN, 256), bf16),
            pltpu.VMEM((OWN, T), f32),
            pltpu.SemaphoreType.DMA((NSEM,)),
            pltpu.SemaphoreType.DMA((NSEM,)),
            pltpu.SemaphoreType.DMA((9,)),
        ],
        compiler_params=pltpu.CompilerParams(
            collective_id=0, has_side_effects=True, vmem_limit_bytes=58 * 1024 * 1024
        ),
    )(
        tokens.T, pre_gain.reshape(42, 128), post_gain.reshape(42, 128), w_qkv, w_o.T, jnp.asarray(rows), jnp.asarray(base),
        page_of.reshape(4, 128), page_start,
    )
    return out.T


def solution(mesh):
    return jax.shard_map(
        per_device,
        mesh=mesh,
        in_specs=(P("ctx", "head"), P(), P(), P("ctx", "head"), P("head", "ctx"), P(), P("ctx")),
        out_specs=P("ctx", "head"),
        check_vma=False,
    )
```
